256 devices in a mesh: tm: 16 (over y, x_hi, core), space: 16 (over x_lo, z).
Axes of the slice: x: 4 (x_hi: 2, x_lo: 2; x = x_hi * 2 + x_lo), y: 4, z: 8, core: 2. Of those that a mesh axis runs over, the one named last changes fastest.
Arguments:
- query: bfloat16 [16, 2048, 1536], P('tm', 'space')
- key_new: bfloat16 [16, 2048, 1536], P('tm', 'space')
- value_new: bfloat16 [16, 2048, 1536], P('tm', 'space'), may hold values from -6 to 6
- key_clean: bfloat16 [16, 2048, 1536], P('tm', 'space'), may hold values from -6 to 6
- value_clean: bfloat16 [16, 2048, 1536], P('tm', 'space'), may hold values from -6 to 6
- out_weight: bfloat16 [1536, 1536], replicated, may hold values from -1.25 to 1.25
- step_gate: float32 [4, 1536], replicated, may hold values from 0.5 to 1.5
- noise_step: int32 [16], P('tm'), may hold values from 0 to 3
- tile_mask: int32 [16, 16, 3], P('tm', 'space'), may hold values 0 or 1
Outputs:
- gated_out: bfloat16 [16, 2048, 1536], P('tm', 'space')
The draws below stay inside these ranges and needn't reach their ends.
All inputs are finite; a program needn't handle non-finite values. No bound on the sum of `tile_mask` on one device may be relied on, other than what follows from the above.
Results may differ from the reference program's by a relative error of at most 0.0075.
Values may be sent and summed in bfloat16 or wider, within the bound.
No kernel may reach another device: no remote copies, remote signals or barrier semaphores. Data moves between devices by JAX's collectives and lax.ppermute only.
A program may use at most 64 MiB of HBM per device.

```python
import math
import jax
import jax.numpy as jnp
from jax import lax

D = 1536
HEADS = 12
HEAD = 128
TILE = 128
PAST = 3
STEPS = 4
GROUPS = 16
TOKC = 2048
TILES = 16


def paired_keys(key):
    return jnp.clip(jax.random.normal(jax.random.fold_in(key, 11), (GROUPS, TOKC, D), jnp.float32), -6.0, 6.0)


def draw_key_new(key, part):
    base = paired_keys(key)
    return base.astype(jnp.bfloat16)


def draw_query(key, part):
    drawn = jnp.clip(1.5 * jax.random.normal(jax.random.fold_in(key, 12), (GROUPS, TOKC, D), jnp.float32), -9.0, 9.0)
    return drawn.astype(jnp.bfloat16)


def with_ends(drawn, stream_key, low, largest):
    dims = drawn.shape
    index_at = [jax.random.randint(jax.random.fold_in(stream_key, axis), (), 0, dims[axis]) for axis in range(len(dims))]
    drawn = drawn.at[tuple(index_at)].set(low)
    longest = dims.index(max(dims))
    index_at[longest] = (index_at[longest] + 1) % dims[longest]
    return drawn.at[tuple(index_at)].set(largest)


def block_levels(key, extent, shards, smallest, high):
    gain = 1.0
    for dim, shards_of in shards:
        draws = jax.random.uniform(jax.random.fold_in(jax.random.fold_in(key, 6), dim), (shards_of,), jnp.float32, smallest / len(shards), high / len(shards))
        gain = gain * jnp.repeat(jnp.exp(draws), extent[dim] // shards_of).reshape((-1,) + (1,) * (len(extent) - 1 - dim))
    return gain


def centred(own_key, dims, spread, bound, split=(), held_as=jnp.bfloat16):
    values = jax.random.normal(own_key, dims, jnp.float32) * spread
    if len(split) > 0:
        values = block_levels(own_key, dims, split, -0.22, 0.18) * values
    return jnp.clip(values, min=-bound, max=bound).astype(held_as)


def setup_inputs(seed: int = 0) -> dict:
    seeds = jax.random.split(jax.random.key(seed), 10)
    return {
        "query": draw_query(jax.random.fold_in(seeds[9], 71), 0),
        "key_new": draw_key_new(jax.random.fold_in(seeds[9], 71), 0),
        "value_new": centred(seeds[2], (GROUPS, TOKC, D), 1.0, 6.0, ((0, 16), (1, 16))),
        "key_clean": centred(seeds[3], (GROUPS, TOKC, D), 1.0, 6.0, ((0, 16), (1, 16))),
        "value_clean": centred(seeds[4], (GROUPS, TOKC, D), 1.0, 6.0, ((0, 16), (1, 16))),
        "out_weight": centred(seeds[5], (D, D), (D // 64) ** -0.5, 1.25),
        "step_gate": jnp.clip(jax.random.uniform(seeds[6], (STEPS, D), jnp.float32, 0.5, 1.5), 0.5, 1.5),
        "noise_step": with_ends(jax.random.randint(seeds[7], (GROUPS,), 0, STEPS), jax.random.fold_in(seeds[7], 1), 0, STEPS - 1).astype(jnp.int32),
        "tile_mask": with_ends((jax.random.randint(seeds[8], (GROUPS, TILES, 3), 0, 3) < 2).astype(jnp.int32), jax.random.fold_in(seeds[8], 1), 0, 1),
    }


def reference(query, key_new, value_new, key_clean, value_clean, out_weight, step_gate, noise_step, tile_mask):
    group_count = query.shape[0]
    token_count = query.shape[1]
    tile_count = token_count // TILE
    score_scale = 1.0 / math.sqrt(HEAD)
    zero = jnp.zeros((), jnp.int32)
    new_keys = jnp.pad(key_new, ((0, 0), (TILE, TILE), (0, 0)))
    new_values = jnp.pad(value_new, ((0, 0), (TILE, TILE), (0, 0)))
    old_keys = jnp.pad(key_clean, ((PAST, 0), (TILE, TILE), (0, 0)))
    old_values = jnp.pad(value_clean, ((PAST, 0), (TILE, TILE), (0, 0)))

    def one_tile(flat_index):
        group = (flat_index // tile_count).astype(jnp.int32)
        tile = (flat_index % tile_count).astype(jnp.int32)
        start = (tile * TILE).astype(jnp.int32)
        query_rows = lax.dynamic_slice(query, (group, start, zero), (1, TILE, D))[0].reshape(TILE, HEADS, HEAD)
        own_keys = lax.dynamic_slice(new_keys, (group, start, zero), (1, 3 * TILE, D))[0]
        own_values = lax.dynamic_slice(new_values, (group, start, zero), (1, 3 * TILE, D))[0]
        past_keys = lax.dynamic_slice(old_keys, (group, start, zero), (PAST, 3 * TILE, D)).reshape(PAST * 3 * TILE, D)
        past_values = lax.dynamic_slice(old_values, (group, start, zero), (PAST, 3 * TILE, D)).reshape(PAST * 3 * TILE, D)
        tile_row = lax.dynamic_slice(tile_mask, (group, tile, zero), (1, 1, 3))[0, 0]
        spots = jnp.arange(3, dtype=jnp.int32)
        target = tile + spots - 1
        tile_ok = ((spots == 1) | (tile_row == 1)) & (target >= 0) & (target < tile_count)
        row_ok = jnp.repeat(tile_ok, TILE)
        past_ok = group - PAST + jnp.arange(PAST, dtype=jnp.int32) >= 0
        key_ok = jnp.concatenate([row_ok, (past_ok[:, None] & row_ok[None, :]).reshape(-1)])
        key_rows = jnp.concatenate([own_keys, past_keys]).reshape(-1, HEADS, HEAD)
        value_rows = jnp.concatenate([own_values, past_values]).reshape(-1, HEADS, HEAD)
        scores = jnp.einsum('qhd,khd->hqk', query_rows.astype(jnp.float32), key_rows.astype(jnp.float32)) * score_scale
        filled = jnp.where(key_ok[None, None, :], scores, -1e+30)
        row_peak = lax.optimization_barrier(jnp.max(filled, axis=-1))
        weights = jnp.where(key_ok[None, None, :], jnp.exp(filled - row_peak[..., None]), 0.0)
        total = lax.optimization_barrier(jnp.sum(weights, axis=-1))
        numer = jnp.einsum('hqk,khd->hqd', weights.astype(jnp.bfloat16).astype(jnp.float32), value_rows.astype(jnp.float32))
        attended = numer / total[..., None]
        return attended.transpose(1, 0, 2).reshape(TILE, D).astype(jnp.bfloat16)
    attended = lax.map(one_tile, jnp.arange(group_count * tile_count, dtype=jnp.int32))
    attended = attended.reshape(group_count * token_count, D)
    projected = jnp.dot(attended, out_weight, preferred_element_type=jnp.float32).reshape(group_count, token_count, D)
    gate_rows = step_gate[noise_step]
    return (gate_rows[:, None, :] * projected).astype(jnp.bfloat16)
```

```python
import functools
import math

import jax
import jax.numpy as jnp
from jax import lax
from jax.experimental import pallas as pl
from jax.experimental.pallas import tpu as pltpu
from jax.sharding import PartitionSpec as P

HEADS = 12
HEAD = 128
TILE = 128
D = HEADS * HEAD
LOG2E = 1.4426950408889634
NEG = -1e30

PARAMS = pltpu.CompilerParams(vmem_limit_bytes=24 * 2**20)


def past_bias(group):
    even = lax.rem(group, 2) == 0
    ok_two = group >= 2
    ok_side = jnp.where(even, group >= 4, group >= 1)
    ok_swap = jnp.where(even, group >= 2, group >= 3)
    return [jnp.where(ok, 0.0, NEG).astype(jnp.float32) for ok in (ok_two, ok_side, ok_swap)]


def head_partial(q, keys, values, biases):
    scale = LOG2E / math.sqrt(HEAD)
    scores = []
    for key, bias in zip(keys, biases):
        s = lax.dot_general(q, key, (((1,), (1,)), ((), ())), preferred_element_type=jnp.float32)
        s = s * scale
        scores.append(s if bias is None else s + bias)
    peak = functools.reduce(jnp.maximum, scores)
    peak = jnp.max(peak, axis=-1, keepdims=True)
    weights = [jnp.exp2(s - peak) for s in scores]
    total = jnp.sum(functools.reduce(jnp.add, weights), axis=-1, keepdims=True)
    w = jnp.concatenate([x.astype(jnp.bfloat16) for x in weights], axis=1)
    v = jnp.concatenate(values, axis=0)
    accum = jnp.dot(w, v, preferred_element_type=jnp.float32)
    return accum * (1.0 / total), peak + jnp.log2(total)


def lanes_of(stats, lse, lane, h):
    return jnp.where(lane == h, lse, stats)


def neighbour_kernel(q_low, q_high, kn, vn, k2, v2, ks, vs, kx, vx, to_low, to_high):
    biases = [None] + past_bias(lax.axis_index("tm"))
    lane = lax.broadcasted_iota(jnp.int32, (2 * TILE, HEAD), 1)
    stats = jnp.zeros((2 * TILE, HEAD), jnp.float32)
    for h in range(HEADS):
        cols = slice(h * HEAD, (h + 1) * HEAD)
        q = jnp.concatenate([q_low[0, :, cols], q_high[0, :, cols]], axis=0)
        keys = [r[0, :, cols] for r in (kn, k2, ks, kx)]
        values = [r[0, :, cols] for r in (vn, v2, vs, vx)]
        part, lse = head_partial(q, keys, values, biases)
        part = part.astype(jnp.bfloat16)
        to_low[:, cols] = part[:TILE]
        to_high[:, cols] = part[TILE:]
        stats = lanes_of(stats, lse, lane, h)
    first = stats.astype(jnp.bfloat16).astype(jnp.float32)
    rest = stats - first
    second = rest.astype(jnp.bfloat16).astype(jnp.float32)
    third = rest - second
    packed = first + pltpu.roll(second, 16, 1) + pltpu.roll(third, 32, 1)
    packed = packed.astype(jnp.bfloat16)
    to_low[:, D:] = packed[:TILE]
    to_high[:, D:] = packed[TILE:]


def own_kernel(q, kn, vn, k2, v2, ks, vs, kx, vx, out, out_lse):
    biases = [None] + past_bias(lax.axis_index("tm"))
    lane = lax.broadcasted_iota(jnp.int32, (TILE, HEAD), 1)
    stats = jnp.zeros((TILE, HEAD), jnp.float32)
    for h in range(HEADS):
        cols = slice(h * HEAD, (h + 1) * HEAD)
        keys = [r[0, :, cols] for r in (kn, k2, ks, kx)]
        values = [r[0, :, cols] for r in (vn, v2, vs, vx)]
        part, lse = head_partial(q[0, :, cols], keys, values, biases)
        out[:, cols] = part
        stats = lanes_of(stats, lse, lane, h)
    out_lse[...] = stats


def unpacked(block):
    packed = block.astype(jnp.float32)
    return packed + pltpu.roll(packed, HEAD - 16, 1) + pltpu.roll(packed, HEAD - 32, 1)


def merge_kernel(
    tiles_all, step, mask, own, own_lse, low, high, weight, gate, out, attended
):
    tile = lax.axis_index("space")
    use_low = (mask[0, 0, 0] == 1) & (tile > 0)
    use_high = (mask[0, 0, 2] == 1) & (tile < tiles_all - 1)
    lse_own = own_lse[...]
    lse_low = jnp.where(use_low, unpacked(low[:, D:]), NEG)
    lse_high = jnp.where(use_high, unpacked(high[:, D:]), NEG)
    peak = jnp.maximum(jnp.maximum(lse_own, lse_low), lse_high)
    w_own = jnp.exp2(lse_own - peak)
    w_low = jnp.exp2(lse_low - peak)
    w_high = jnp.exp2(lse_high - peak)
    inv = 1.0 / (w_own + w_low + w_high)
    w_own, w_low, w_high = w_own * inv, w_low * inv, w_high * inv
    for h in range(HEADS):
        cols = slice(h * HEAD, (h + 1) * HEAD)
        one = slice(h, h + 1)
        mixed = (
            w_own[:, one] * own[:, cols]
            + w_low[:, one] * low[:, cols].astype(jnp.float32)
            + w_high[:, one] * high[:, cols].astype(jnp.float32)
        )
        attended[:, cols] = mixed.astype(jnp.bfloat16)
    gate_row = gate[pl.ds(step[0], 1), :]
    att = attended[...]
    for n in range(0, D, 256):
        cols = slice(n, n + 256)
        projected = jnp.dot(att, weight[:, cols], preferred_element_type=jnp.float32)
        out[0, :, cols] = (gate_row[:, cols] * projected).astype(jnp.bfloat16)


VMEM = pl.BlockSpec(memory_space=pltpu.VMEM)
SMEM = pl.BlockSpec(memory_space=pltpu.SMEM)


def on_device(
    tm_size,
    space_size,
    query,
    key_new,
    value_new,
    key_clean,
    value_clean,
    out_weight,
    step_gate,
    noise_step,
    tile_mask,
):
    two_back = [(t, t + 2) for t in range(tm_size - 2)]
    side = [(t, t + 1 if t % 2 == 0 else t + 3) for t in range(tm_size)]
    side = [(a, b) for a, b in side if b < tm_size]
    swap = [(t, t + 1 if t % 2 == 0 else t - 1) for t in range(tm_size)]
    up = [(s, s + 1) for s in range(space_size - 1)]
    down = [(b, a) for a, b in up]

    k2 = lax.ppermute(key_clean, "tm", two_back)
    v2 = lax.ppermute(value_clean, "tm", two_back)
    q_low = lax.ppermute(query, "space", up)
    q_high = lax.ppermute(query, "space", down)
    ks = lax.ppermute(key_clean, "tm", side)
    vs = lax.ppermute(value_clean, "tm", side)
    kx = lax.ppermute(k2, "tm", swap)
    vx = lax.ppermute(v2, "tm", swap)

    key_args = (key_new, value_new, k2, v2, ks, vs, kx, vx)
    width = D + HEAD
    to_low, to_high = pl.pallas_call(
        neighbour_kernel,
        out_shape=(jax.ShapeDtypeStruct((TILE, width), jnp.bfloat16),) * 2,
        in_specs=[VMEM] * 10,
        out_specs=(VMEM, VMEM),
        cost_estimate=pl.CostEstimate(
            flops=4 * 256 * 512 * D, bytes_accessed=12 * TILE * D * 2, transcendentals=HEADS * 256 * 512
        ),
        name="neighbour",
        compiler_params=PARAMS,
    )(q_low, q_high, *key_args)
    from_high = lax.ppermute(to_low, "space", down)
    from_low = lax.ppermute(to_high, "space", up)

    own, own_lse = pl.pallas_call(
        own_kernel,
        out_shape=(
            jax.ShapeDtypeStruct((TILE, D), jnp.float32),
            jax.ShapeDtypeStruct((TILE, HEAD), jnp.float32),
        ),
        in_specs=[VMEM] * 9,
        out_specs=(VMEM, VMEM),
        cost_estimate=pl.CostEstimate(
            flops=4 * 128 * 512 * D, bytes_accessed=12 * TILE * D * 2, transcendentals=HEADS * 128 * 512
        ),
        name="own",
        compiler_params=PARAMS,
    )(query, *key_args)

    return pl.pallas_call(
        functools.partial(merge_kernel, space_size),
        out_shape=jax.ShapeDtypeStruct((1, TILE, D), jnp.bfloat16),
        in_specs=[SMEM, SMEM] + [VMEM] * 6,
        out_specs=VMEM,
        scratch_shapes=[pltpu.VMEM((TILE, D), jnp.bfloat16)],
        cost_estimate=pl.CostEstimate(
            flops=2 * TILE * D * D, bytes_accessed=2 * D * D + 8 * TILE * D, transcendentals=0
        ),
        name="merge",
        compiler_params=PARAMS,
    )(noise_step, tile_mask, own, own_lse, from_low, from_high, out_weight, step_gate)


def solution(mesh):
    placed = (
        P("tm", "space", None),
        P("tm", "space", None),
        P("tm", "space", None),
        P("tm", "space", None),
        P("tm", "space", None),
        P(),
        P(),
        P("tm"),
        P("tm", "space", None),
    )
    body = functools.partial(on_device, mesh.shape["tm"], mesh.shape["space"])
    return jax.shard_map(
        body, mesh=mesh, in_specs=placed, out_specs=P("tm", "space", None), check_vma=False
    )
```

```python
import functools
import math

import jax
import jax.numpy as jnp
from jax import lax
from jax.experimental import pallas as pl
from jax.experimental.pallas import tpu as pltpu
from jax.sharding import PartitionSpec as P


HEADS = 12
HEAD = 128
TILE = 128
D = HEADS * HEAD
LOG2E = 1.4426950408889634
NEG = -1e30

PARAMS = pltpu.CompilerParams(vmem_limit_bytes=24 * 2**20)


def past_bias(group):
    even = lax.rem(group, 2) == 0
    ok_two = group >= 2
    ok_side = jnp.where(even, group >= 4, group >= 1)
    ok_swap = jnp.where(even, group >= 2, group >= 3)
    return [jnp.where(ok, 0.0, NEG).astype(jnp.float32) for ok in (ok_two, ok_side, ok_swap)]


def head_partial(q, keys, values, biases):
    scale = LOG2E / math.sqrt(HEAD)
    scores = []
    for key, bias in zip(keys, biases):
        s = lax.dot_general(q, key, (((1,), (1,)), ((), ())), preferred_element_type=jnp.float32)
        s = s * scale
        scores.append(s if bias is None else s + bias)
    peak = functools.reduce(jnp.maximum, scores)
    peak = jnp.max(peak, axis=-1, keepdims=True)
    weights = [jnp.exp2(s - peak) for s in scores]
    total = jnp.sum(functools.reduce(jnp.add, weights), axis=-1, keepdims=True)
    w = jnp.concatenate([x.astype(jnp.bfloat16) for x in weights], axis=1)
    v = jnp.concatenate(values, axis=0)
    accum = jnp.dot(w, v, preferred_element_type=jnp.float32)
    return accum * (1.0 / total), peak + jnp.log2(total)


def chunk_blocks(h, blocks):
    cols = slice(h * HEAD, (h + 1) * HEAD)
    return cols, [r[0, :, cols] for r in blocks[0::2]], [r[0, :, cols] for r in blocks[1::2]]


def stage_kernel(tiles_all, step, mask, gate, q, kn, vn, q_out, kn_out, vn_out, gate_out, bias_out, sems):
    copies = [
        pltpu.make_async_copy(source, target, sems.at[i])
        for i, (source, target) in enumerate(((q, q_out), (kn, kn_out), (vn, vn_out)))
    ]
    for copy in copies:
        copy.start()
    gate_out[...] = gate[pl.ds(step[0], 1), :]
    tile = lax.axis_index("space")
    even = lax.rem(tile, 2) == 0
    use_low = (mask[0, 0, 0] == 1) & (tile > 0)
    use_high = (mask[0, 0, 2] == 1) & (tile < tiles_all - 1)
    zero = jnp.zeros((1, HEAD), jnp.float32)
    low = jnp.where(use_low, zero, NEG)
    high = jnp.where(use_high, zero, NEG)
    bias_out[0:1, :] = jnp.where(even, high, low)
    bias_out[1:2, :] = jnp.where(even, low, high)
    for copy in copies:
        copy.wait()


def neighbour_kernel(first, heads, q_one, q_two, *refs):
    blocks, (to_one, to_two) = refs[:8], refs[8:]
    biases = [None] + past_bias(lax.axis_index("tm"))
    lane = lax.broadcasted_iota(jnp.int32, (2 * TILE, HEAD), 1)
    stats = jnp.zeros((2 * TILE, HEAD), jnp.float32)
    width = heads * HEAD
    for h in range(heads):
        cols, keys, values = chunk_blocks(first + h, blocks)
        q = jnp.concatenate([q_one[0, :, cols], q_two[0, :, cols]], axis=0)
        part, lse = head_partial(q, keys, values, biases)
        part = part.astype(jnp.bfloat16)
        here = slice(h * HEAD, (h + 1) * HEAD)
        to_one[:, here] = part[:TILE]
        to_two[:, here] = part[TILE:]
        stats = jnp.where(lane == h, lse, stats)
    first_part = stats.astype(jnp.bfloat16).astype(jnp.float32)
    rest = stats - first_part
    second_part = rest.astype(jnp.bfloat16).astype(jnp.float32)
    third_part = rest - second_part
    packed = first_part + pltpu.roll(second_part, 16, 1) + pltpu.roll(third_part, 32, 1)
    packed = packed.astype(jnp.bfloat16)
    to_one[:, width:] = packed[:TILE]
    to_two[:, width:] = packed[TILE:]


def own_kernel(first, heads, q, *refs):
    blocks, (out, out_lse) = refs[:8], refs[8:]
    biases = [None] + past_bias(lax.axis_index("tm"))
    lane = lax.broadcasted_iota(jnp.int32, (TILE, HEAD), 1)
    stats = jnp.zeros((TILE, HEAD), jnp.float32)
    for h in range(heads):
        cols, keys, values = chunk_blocks(first + h, blocks)
        part, lse = head_partial(q[0, :, cols], keys, values, biases)
        out[:, h * HEAD : (h + 1) * HEAD] = part
        stats = jnp.where(lane == h, lse, stats)
    out_lse[...] = stats


def unpacked(block):
    packed = block.astype(jnp.float32)
    return packed + pltpu.roll(packed, HEAD - 16, 1) + pltpu.roll(packed, HEAD - 32, 1)


def merge_kernel(first, heads, has_sum, last, bias, own, own_lse, one, two, weight, *rest):
    rest = list(rest)
    gate = rest.pop(0) if last else None
    before = rest.pop(0) if has_sum else None
    out, attended = rest
    width = heads * HEAD
    lse_own = own_lse[...]
    lse_one = unpacked(one[:, width:]) + bias[0:1, :]
    lse_two = unpacked(two[:, width:]) + bias[1:2, :]
    peak = jnp.maximum(jnp.maximum(lse_own, lse_one), lse_two)
    w_own = jnp.exp2(lse_own - peak)
    w_one = jnp.exp2(lse_one - peak)
    w_two = jnp.exp2(lse_two - peak)
    inv = 1.0 / (w_own + w_one + w_two)
    w_own, w_one, w_two = w_own * inv, w_one * inv, w_two * inv
    for h in range(heads):
        cols = slice(h * HEAD, (h + 1) * HEAD)
        lane = slice(h, h + 1)
        mixed = (
            w_own[:, lane] * own[:, cols]
            + w_one[:, lane] * one[:, cols].astype(jnp.float32)
            + w_two[:, lane] * two[:, cols].astype(jnp.float32)
        )
        attended[:, cols] = mixed.astype(jnp.bfloat16)
    att = attended[...]
    rows = slice(first * HEAD, first * HEAD + width)
    for n in range(0, D, 256):
        cols = slice(n, n + 256)
        projected = jnp.dot(att, weight[rows, cols], preferred_element_type=jnp.float32)
        if has_sum:
            projected = projected + before[:, cols]
        if last:
            out[0, :, cols] = (gate[:, cols] * projected).astype(jnp.bfloat16)
        else:
            out[:, cols] = projected


VMEM = pl.BlockSpec(memory_space=pltpu.VMEM)
SMEM = pl.BlockSpec(memory_space=pltpu.SMEM)
HBM = pl.BlockSpec(memory_space=pltpu.HBM)
CHUNKS = ((0, 8), (8, 4))


def cost(flops, moved, exps=0):
    return pl.CostEstimate(flops=flops, bytes_accessed=moved, transcendentals=exps)


def stage(space_size, noise_step, tile_mask, step_gate, query, key_new, value_new):
    block = jax.ShapeDtypeStruct((1, TILE, D), jnp.bfloat16)
    return pl.pallas_call(
        functools.partial(stage_kernel, space_size),
        out_shape=(
            block,
            block,
            block,
            jax.ShapeDtypeStruct((1, D), jnp.float32),
            jax.ShapeDtypeStruct((8, HEAD), jnp.float32),
        ),
        in_specs=[SMEM, SMEM, VMEM, HBM, HBM, HBM],
        out_specs=(VMEM,) * 5,
        scratch_shapes=[pltpu.SemaphoreType.DMA((3,))],
        cost_estimate=cost(0, 12 * TILE * D),
        compiler_params=PARAMS,
        name="stage",
    )(noise_step, tile_mask, step_gate, *in_hbm(query, key_new, value_new))


def neighbour(first, heads, *args):
    width = heads * HEAD
    return pl.pallas_call(
        functools.partial(neighbour_kernel, first, heads),
        out_shape=(jax.ShapeDtypeStruct((TILE, width + HEAD), jnp.bfloat16),) * 2,
        in_specs=[VMEM] * 10,
        out_specs=(VMEM, VMEM),
        cost_estimate=cost(4 * 256 * 512 * width, 24 * TILE * width, heads * 256 * 512),
        compiler_params=PARAMS,
    )(*args)


def own(first, heads, *args):
    width = heads * HEAD
    return pl.pallas_call(
        functools.partial(own_kernel, first, heads),
        out_shape=(
            jax.ShapeDtypeStruct((TILE, width), jnp.float32),
            jax.ShapeDtypeStruct((TILE, HEAD), jnp.float32),
        ),
        in_specs=[VMEM] * 9,
        out_specs=(VMEM, VMEM),
        cost_estimate=cost(4 * 128 * 512 * width, 22 * TILE * width, heads * 128 * 512),
        compiler_params=PARAMS,
    )(*args)


def merge(first, heads, has_sum, last, *args):
    width = heads * HEAD
    if last:
        result = jax.ShapeDtypeStruct((1, TILE, D), jnp.bfloat16)
    else:
        result = jax.ShapeDtypeStruct((TILE, D), jnp.float32)
    return pl.pallas_call(
        functools.partial(merge_kernel, first, heads, has_sum, last),
        out_shape=result,
        in_specs=[VMEM] * len(args),
        out_specs=VMEM,
        scratch_shapes=[pltpu.VMEM((TILE, width), jnp.bfloat16)],
        cost_estimate=cost(2 * TILE * D * width, 2 * D * width + 8 * TILE * D),
        compiler_params=PARAMS,
    )(*args)


def in_hbm(*arrays):
    return [pltpu.with_memory_space_constraint(a, pltpu.HBM) for a in arrays]


def on_device(
    tm_size,
    space_size,
    query,
    key_new,
    value_new,
    key_clean,
    value_clean,
    out_weight,
    step_gate,
    noise_step,
    tile_mask,
):
    two_back = [(t, (t + 2) % tm_size) for t in range(tm_size)]
    side = [(t, (t + (1 if t % 2 == 0 else 3)) % tm_size) for t in range(tm_size)]
    swap = [(t, t + 1 if t % 2 == 0 else t - 1) for t in range(tm_size)]

    one = [(s, s + 1 if s % 2 == 0 else s - 1) for s in range(space_size)]
    two = []
    for t in range(tm_size):
        for s in range(space_size):
            to = s - 1 if s % 2 == 0 else s + 1
            inside = 0 <= to < space_size
            target = (t, to) if inside else (swap[t][1], s)
            two.append((t * space_size + s, target[0] * space_size + target[1]))
    both = ("tm", "space")

    k2 = lax.ppermute(key_clean, "tm", two_back)
    v2 = lax.ppermute(value_clean, "tm", two_back)
    ks = lax.ppermute(key_clean, "tm", side)
    vs = lax.ppermute(value_clean, "tm", side)
    q_one = lax.ppermute(query, "space", one)
    q_two = lax.ppermute(query, both, two)
    kx = lax.ppermute(k2, "tm", swap)
    vx = lax.ppermute(v2, "tm", swap)
    q, kn, vn, gate_row, bias = stage(
        space_size, noise_step, tile_mask, step_gate, query, key_new, value_new
    )
    blocks = (kn, vn, k2, v2, ks, vs, kx, vx)
    total = None
    for i, (first, heads) in enumerate(CHUNKS):
        to_one, to_two = neighbour(first, heads, q_one, q_two, *blocks)
        from_one = lax.ppermute(to_one, "space", one)
        from_two = lax.ppermute(to_two, both, two)
        mine, mine_lse = own(first, heads, q, *blocks)
        last = i == len(CHUNKS) - 1
        args = [bias, mine, mine_lse, from_one, from_two, out_weight]
        args += [gate_row] if last else []
        args += [total] if i > 0 else []
        total = merge(first, heads, i > 0, last, *args)
    return total


def solution(mesh):
    placed = (
        P("tm", "space", None),
        P("tm", "space", None),
        P("tm", "space", None),
        P("tm", "space", None),
        P("tm", "space", None),
        P(),
        P(),
        P("tm"),
        P("tm", "space", None),
    )
    body = functools.partial(on_device, mesh.shape["tm"], mesh.shape["space"])
    return jax.shard_map(
        body, mesh=mesh, in_specs=placed, out_specs=P("tm", "space", None), check_vma=False
    )
```

```python
import functools
import math

import jax
import jax.numpy as jnp
from jax import lax
from jax.experimental import pallas as pl
from jax.experimental.pallas import tpu as pltpu
from jax.sharding import PartitionSpec as P


HEADS = 12
HEAD = 128
TILE = 128
D = HEADS * HEAD
LOG2E = 1.4426950408889634
NEG = -1e30

PARAMS = pltpu.CompilerParams(vmem_limit_bytes=24 * 2**20)


def past_bias(group):
    even = lax.rem(group, 2) == 0
    ok_two = group >= 2
    ok_side = jnp.where(even, group >= 4, group >= 1)
    ok_swap = jnp.where(even, group >= 2, group >= 3)
    return [jnp.where(ok, 0.0, NEG).astype(jnp.float32) for ok in (ok_two, ok_side, ok_swap)]


def head_partial(q, keys, values, biases):
    scale = LOG2E / math.sqrt(HEAD)
    scores = []
    for key, bias in zip(keys, biases):
        s = lax.dot_general(q, key, (((1,), (1,)), ((), ())), preferred_element_type=jnp.float32)
        s = s * scale
        scores.append(s if bias is None else s + bias)
    peak = functools.reduce(jnp.maximum, scores)
    peak = jnp.max(peak, axis=-1, keepdims=True)
    weights = [jnp.exp2(s - peak) for s in scores]
    total = jnp.sum(functools.reduce(jnp.add, weights), axis=-1, keepdims=True)
    w = jnp.concatenate([x.astype(jnp.bfloat16) for x in weights], axis=1)
    v = jnp.concatenate(values, axis=0)
    accum = jnp.dot(w, v, preferred_element_type=jnp.float32)
    return accum * (1.0 / total), peak + jnp.log2(total)


def chunk_blocks(first, heads, h, kn, vn, packs):
    cols = slice((first + h) * HEAD, (first + h + 1) * HEAD)
    key_cols = slice(h * HEAD, (h + 1) * HEAD)
    value_cols = slice((heads + h) * HEAD, (heads + h + 1) * HEAD)
    keys = [kn[0, :, cols]] + [p[:, key_cols] for p in packs]
    values = [vn[0, :, cols]] + [p[:, value_cols] for p in packs]
    return cols, keys, values


def pack_kernel(first, heads, key, value, out, sems):
    width = heads * HEAD
    rows = TILE // PACK_PARTS
    copies = []
    for part in range(PACK_PARTS):
        for i, source in enumerate((key, value)):
            copies.append(
                pltpu.make_async_copy(
                    source.at[0, pl.ds(part * rows, rows), pl.ds(first * HEAD, width)],
                    out.at[pl.ds(part * rows, rows), pl.ds(i * width, width)],
                    sems.at[part, i],
                )
            )
    for copy in copies:
        copy.start()
    for copy in copies:
        copy.wait()


def stage_kernel(tiles_all, step, mask, gate, q, kn, vn, q_out, kn_out, vn_out, gate_out, bias_out, sems):
    copies = [
        pltpu.make_async_copy(source, target, sems.at[i])
        for i, (source, target) in enumerate(((q, q_out), (kn, kn_out), (vn, vn_out)))
    ]
    for copy in copies:
        copy.start()
    gate_out[...] = gate[pl.ds(step[0], 1), :]
    tile = lax.axis_index("space")
    even = lax.rem(tile, 2) == 0
    use_low = (mask[0, 0, 0] == 1) & (tile > 0)
    use_high = (mask[0, 0, 2] == 1) & (tile < tiles_all - 1)
    zero = jnp.zeros((1, HEAD), jnp.float32)
    low = jnp.where(use_low, zero, NEG)
    high = jnp.where(use_high, zero, NEG)
    bias_out[0:1, :] = jnp.where(even, high, low)
    bias_out[1:2, :] = jnp.where(even, low, high)
    for copy in copies:
        copy.wait()


def at_meeting(half):
    tile = lax.axis_index("space")
    odd = lax.rem(lax.axis_index("tm"), 2) == 1
    return odd & ((tile == half - 1) | (tile == half))


def neighbour_kernel(half, first, heads, q_one, q_two, q_meet, kn, vn, *refs):
    packs, (to_one, to_two) = refs[:3], refs[3:]
    biases = [None] + past_bias(lax.axis_index("tm"))
    lane = lax.broadcasted_iota(jnp.int32, (2 * TILE, HEAD), 1)
    stats = jnp.zeros((2 * TILE, HEAD), jnp.float32)
    meeting = at_meeting(half)
    for h in range(heads):
        cols, keys, values = chunk_blocks(first, heads, h, kn, vn, packs)
        second = jnp.where(meeting, q_meet[0, :, cols], q_two[0, :, cols])
        q = jnp.concatenate([q_one[0, :, cols], second], axis=0)
        part, lse = head_partial(q, keys, values, biases)
        part = part.astype(jnp.bfloat16)
        here = slice(h * HEAD, (h + 1) * HEAD)
        to_one[:TILE, here] = part[:TILE]
        to_two[:TILE, here] = part[TILE:]
        stats = jnp.where(lane == h, lse, stats)
    first_part = stats.astype(jnp.bfloat16).astype(jnp.float32)
    rest = stats - first_part
    second_part = rest.astype(jnp.bfloat16).astype(jnp.float32)
    third_part = rest - second_part
    packed = first_part + pltpu.roll(second_part, 8, 1) + pltpu.roll(third_part, 16, 1)
    for target, block in ((to_one, packed[:TILE]), (to_two, packed[TILE:])):
        turned = block.T.astype(jnp.bfloat16)
        for part in range(3):
            target[TILE:, part * HEAD : (part + 1) * HEAD] = turned[part * 8 : (part + 1) * 8]
        for part in range(3, heads):
            target[TILE:, part * HEAD : (part + 1) * HEAD] = jnp.zeros((8, HEAD), jnp.bfloat16)


def own_kernel(first, heads, start, count, q, kn, vn, *refs):
    packs, (out, out_lse) = refs[:3], refs[3:]
    biases = [None] + past_bias(lax.axis_index("tm"))
    lane = lax.broadcasted_iota(jnp.int32, (TILE, HEAD), 1)
    stats = jnp.zeros((TILE, HEAD), jnp.float32)
    for h in range(start, start + count):
        cols, keys, values = chunk_blocks(first, heads, h, kn, vn, packs)
        part, lse = head_partial(q[0, :, cols], keys, values, biases)
        out[:, (h - start) * HEAD : (h - start + 1) * HEAD] = part
        stats = jnp.where(lane == h, lse, stats)
    out_lse[...] = stats


def unpacked(rows):
    parts = rows.astype(jnp.float32)
    lse = parts[:, :HEAD] + parts[:, HEAD : 2 * HEAD] + parts[:, 2 * HEAD : 3 * HEAD]
    return jnp.concatenate([lse, jnp.zeros((HEAD - 8, HEAD), jnp.float32)], axis=0).T


def merge_kernel(first, heads, parts, has_sum, last, bias, one, two, weight, *rest):
    rest = list(rest)
    own = [rest.pop(0) for _ in range(parts)]
    own_lse = [rest.pop(0) for _ in range(parts)]
    gate = rest.pop(0) if last else None
    before = rest.pop(0) if has_sum else None
    out, attended = rest
    width = heads * HEAD
    lse_own = functools.reduce(jnp.add, [r[...] for r in own_lse])
    lse_one = unpacked(one[TILE:, : 3 * HEAD]) + bias[0:1, :]
    lse_two = unpacked(two[TILE:, : 3 * HEAD]) + bias[1:2, :]
    peak = jnp.maximum(jnp.maximum(lse_own, lse_one), lse_two)
    w_own = jnp.exp2(lse_own - peak)
    w_one = jnp.exp2(lse_one - peak)
    w_two = jnp.exp2(lse_two - peak)
    inv = 1.0 / (w_own + w_one + w_two)
    w_own, w_one, w_two = w_own * inv, w_one * inv, w_two * inv
    count = heads // parts
    for h in range(heads):
        cols = slice(h * HEAD, (h + 1) * HEAD)
        lane = slice(h, h + 1)
        mixed = (
            w_own[:, lane] * own[h // count][:, (h % count) * HEAD : (h % count + 1) * HEAD]
            + w_one[:, lane] * one[:TILE, cols].astype(jnp.float32)
            + w_two[:, lane] * two[:TILE, cols].astype(jnp.float32)
        )
        attended[:, cols] = mixed.astype(jnp.bfloat16)
    att = attended[...]
    rows = slice(first * HEAD, first * HEAD + width)
    for n in range(0, D, 256):
        cols = slice(n, n + 256)
        projected = jnp.dot(att, weight[rows, cols], preferred_element_type=jnp.float32)
        if has_sum:
            projected = projected + before[:, cols]
        if last:
            out[0, :, cols] = (gate[:, cols] * projected).astype(jnp.bfloat16)
        else:
            out[:, cols] = projected


VMEM = pl.BlockSpec(memory_space=pltpu.VMEM)
SMEM = pl.BlockSpec(memory_space=pltpu.SMEM)
HBM = pl.BlockSpec(memory_space=pltpu.HBM)
CHUNKS = ((0, 8), (8, 4))
OWN_PARTS = (2, 1)
PACK_PARTS = 1


def cost(flops, moved, exps=0):
    return pl.CostEstimate(flops=flops, bytes_accessed=moved, transcendentals=exps)


def pack(first, heads, key, value):
    return pl.pallas_call(
        functools.partial(pack_kernel, first, heads),
        out_shape=jax.ShapeDtypeStruct((TILE, 2 * heads * HEAD), jnp.bfloat16),
        in_specs=[HBM, HBM],
        out_specs=VMEM,
        scratch_shapes=[pltpu.SemaphoreType.DMA((PACK_PARTS, 2))],
        cost_estimate=cost(0, 8 * TILE * heads * HEAD),
        compiler_params=PARAMS,
    )(*in_hbm(key, value))


def stage(space_size, noise_step, tile_mask, step_gate, query, key_new, value_new):
    block = jax.ShapeDtypeStruct((1, TILE, D), jnp.bfloat16)
    return pl.pallas_call(
        functools.partial(stage_kernel, space_size),
        out_shape=(
            block,
            block,
            block,
            jax.ShapeDtypeStruct((1, D), jnp.float32),
            jax.ShapeDtypeStruct((8, HEAD), jnp.float32),
        ),
        in_specs=[SMEM, SMEM, VMEM, HBM, HBM, HBM],
        out_specs=(VMEM,) * 5,
        scratch_shapes=[pltpu.SemaphoreType.DMA((3,))],
        cost_estimate=cost(0, 12 * TILE * D),
        compiler_params=PARAMS,
        name="stage",
    )(noise_step, tile_mask, step_gate, *in_hbm(query, key_new, value_new))


def neighbour(half, first, heads, *args):
    width = heads * HEAD
    return pl.pallas_call(
        functools.partial(neighbour_kernel, half, first, heads),
        out_shape=(jax.ShapeDtypeStruct((TILE + 8, width), jnp.bfloat16),) * 2,
        in_specs=[VMEM] * 8,
        out_specs=(VMEM, VMEM),
        cost_estimate=cost(4 * 256 * 512 * width, 24 * TILE * width, heads * 256 * 512),
        compiler_params=PARAMS,
    )(*args)


def own(first, heads, start, count, *args):
    width = count * HEAD
    return pl.pallas_call(
        functools.partial(own_kernel, first, heads, start, count),
        out_shape=(
            jax.ShapeDtypeStruct((TILE, width), jnp.float32),
            jax.ShapeDtypeStruct((TILE, HEAD), jnp.float32),
        ),
        in_specs=[VMEM] * 6,
        out_specs=(VMEM, VMEM),
        cost_estimate=cost(4 * 128 * 512 * width, 22 * TILE * width, count * 128 * 512),
        compiler_params=PARAMS,
    )(*args)


def merge(first, heads, parts, has_sum, last, *args):
    width = heads * HEAD
    if last:
        result = jax.ShapeDtypeStruct((1, TILE, D), jnp.bfloat16)
    else:
        result = jax.ShapeDtypeStruct((TILE, D), jnp.float32)
    return pl.pallas_call(
        functools.partial(merge_kernel, first, heads, parts, has_sum, last),
        out_shape=result,
        in_specs=[VMEM] * len(args),
        out_specs=VMEM,
        scratch_shapes=[pltpu.VMEM((TILE, width), jnp.bfloat16)],
        cost_estimate=cost(2 * TILE * D * width, 2 * D * width + 8 * TILE * D),
        compiler_params=PARAMS,
    )(*args)


def in_hbm(*arrays):
    return [pltpu.with_memory_space_constraint(a, pltpu.HBM) for a in arrays]


def on_device(
    tm_size,
    space_size,
    query,
    key_new,
    value_new,
    key_clean,
    value_clean,
    out_weight,
    step_gate,
    noise_step,
    tile_mask,
):
    two_back = [(t, (t + 2) % tm_size) for t in range(tm_size)]
    side = [(t, (t + (1 if t % 2 == 0 else 3)) % tm_size) for t in range(tm_size)]
    swap = [(t, t + 1 if t % 2 == 0 else t - 1) for t in range(tm_size)]

    one = [(s, s + 1 if s % 2 == 0 else s - 1) for s in range(space_size)]
    two = []
    for t in range(tm_size):
        for s in range(space_size):
            to = s - 1 if s % 2 == 0 else s + 1
            inside = 0 <= to < space_size
            target = (t, to) if inside else (swap[t][1], s)
            two.append((t * space_size + s, target[0] * space_size + target[1]))
    both = ("tm", "space")
    half = space_size // 2
    low, high, end = half - 1, half, space_size - 1
    hop = {divmod(a, space_size): divmod(b, space_size) for a, b in two}
    across = {}
    for t in range(tm_size):
        for s in range(space_size):
            across[t, s] = (swap[t][1], s)
    for t in range(0, tm_size, 2):
        hop[t, 0], hop[t, end] = (t + 1, low), (t + 1, high)
        hop[t + 1, 0], hop[t + 1, end] = (t, 0), (t, end)
        hop[t + 1, low], hop[t + 1, high] = (t + 1, 0), (t + 1, end)
        across[t + 1, 0], across[t + 1, end] = (t + 1, high), (t + 1, low)
        across[t, low], across[t, high] = (t, 0), (t, end)
    hop = [(a[0] * space_size + a[1], b[0] * space_size + b[1]) for a, b in hop.items()]
    across = [(a[0] * space_size + a[1], b[0] * space_size + b[1]) for a, b in across.items()]

    crossing = []
    for first, heads in CHUNKS:
        packed = pack(first, heads, key_clean, value_clean)
        pair = lax.ppermute(packed, "tm", two_back), lax.ppermute(packed, "tm", side)
        crossing.append(pair)
    q_one = lax.ppermute(query, "space", one)
    q_two = lax.ppermute(query, both, hop)
    q_meet = lax.ppermute(q_two, both, across)
    q, kn, vn, gate_row, bias = stage(
        space_size, noise_step, tile_mask, step_gate, query, key_new, value_new
    )
    total = None
    for i, (first, heads) in enumerate(CHUNKS):
        two_ago, aside = crossing[i]
        swapped = lax.ppermute(two_ago, "tm", swap)
        blocks = (kn, vn, two_ago, aside, swapped)
        to_one, to_two = neighbour(half, first, heads, q_one, q_two, q_meet, *blocks)
        from_one = lax.ppermute(to_one, "space", one)
        last = i == len(CHUNKS) - 1
        from_two = lax.ppermute(to_two, both, two)
        parts = OWN_PARTS[i]
        mine = []
        for j in range(parts):
            count = heads // parts
            mine.append(own(first, heads, j * count, count, q, *blocks))
        last = i == len(CHUNKS) - 1
        args = [bias, from_one, from_two, out_weight]
        args += [m[0] for m in mine] + [m[1] for m in mine]
        args += [gate_row] if last else []
        args += [total] if i > 0 else []
        total = merge(first, heads, parts, i > 0, last, *args)
    return total


def solution(mesh):
    placed = (
        P("tm", "space", None),
        P("tm", "space", None),
        P("tm", "space", None),
        P("tm", "space", None),
        P("tm", "space", None),
        P(),
        P(),
        P("tm"),
        P("tm", "space", None),
    )
    body = functools.partial(on_device, mesh.shape["tm"], mesh.shape["space"])
    return jax.shard_map(
        body, mesh=mesh, in_specs=placed, out_specs=P("tm", "space", None), check_vma=False
    )
```
